32 devices in a mesh: replica: 8 (over z, y), fsdp: 4 (over x, core).
Axes of the slice: x: 2, y: 2, z: 4, core: 2. Of those that a mesh axis runs over, the one named last changes fastest.
Arguments:
- tokens: bfloat16 [8, 512, 4096], P('replica', 'fsdp'), may hold values from -6 to 6
- local_weight: bfloat16 [8, 4096, 512], P('replica', 'fsdp'), may hold values from -6 to 6
- key_cot: bfloat16 [8, 512, 512], P('replica', 'fsdp'), may hold values from -6 to 6
- global_weight: float32 [4096, 512], P(('fsdp', 'replica')), may hold values from -6 to 6
- momentum: float32 [4096, 512], P(('fsdp', 'replica')), may hold values from -6 to 6
- anchor: float32 [4096, 512], P(('fsdp', 'replica')), may hold values from -6 to 6
Outputs:
- keys: bfloat16 [8, 512, 512], P('replica', 'fsdp')
- grad_tokens: bfloat16 [8, 512, 4096], P('replica', 'fsdp')
- grad_weight: bfloat16 [8, 4096, 512], P('replica', 'fsdp')
- momentum_new: float32 [4096, 512], P(('fsdp', 'replica'))
- global_new: float32 [4096, 512], P(('fsdp', 'replica'))
- synced: bfloat16 [4096, 512], P('fsdp')
The draws below stay inside these ranges and needn't reach their ends.
All inputs are finite; a program needn't handle non-finite values.
Results may differ from the reference program's by a relative error of at most 0.0095.
Values may be sent and summed in bfloat16 or wider, within the bound.
No kernel may reach another device: no remote copies, remote signals or barrier semaphores. Data moves between devices by JAX's collectives and lax.ppermute only.
A program may use at most 64 MiB of HBM per device.

```python
import jax
import jax.numpy as jnp
from jax import lax

D_WIN = 4096
KVW = 512
TOK_R = 512
N_REPLICA = 8


def strengthened(values, stream_key, source, target, shards_of, factor):
    owner, partner = [(jnp.arange(values.shape[dim]) // (values.shape[dim] // shards_of)).reshape([-1 if axis == dim else 1 for axis in range(values.ndim)]) for dim in (source, target)]
    chosen = jax.random.permutation(stream_key, shards_of)[partner]
    strong = (owner == chosen) | (owner == (partner + shards_of // 2) % shards_of)
    return jnp.where(strong, factor * values, values)


def block_levels(key, extent, cuts, least, largest):
    factor_of = 1.0
    for axis_at, parts in cuts:
        heights = jax.random.uniform(jax.random.fold_in(jax.random.fold_in(key, 6), axis_at), (parts,), jnp.float32, least / len(cuts), largest / len(cuts))
        factor_of = factor_of * jnp.repeat(jnp.exp(heights), extent[axis_at] // parts).reshape((-1,) + (1,) * (len(extent) - 1 - axis_at))
    return factor_of


def scatter_about(stream_key, shape, width, bound, shards=(), held_as=jnp.bfloat16):
    array = width * jax.random.normal(stream_key, shape, jnp.float32)
    if shards:
        array = array * block_levels(stream_key, shape, shards, -0.22, 0.18)
    return jnp.clip(array, -bound, bound).astype(held_as)


def bell_draw_with(stream_key, dims, scale, most, shards, heavy, held_as=jnp.bfloat16):
    values = scale * jax.random.normal(stream_key, dims, jnp.float32)
    if shards:
        values = values * block_levels(stream_key, dims, shards, -0.22, 0.18)
    return jnp.clip(strengthened(values, jax.random.fold_in(stream_key, 3), *heavy), -most, most).astype(held_as)


def setup_inputs(seed: int = 0) -> dict:
    arg_keys = jax.random.split(jax.random.key(seed), 7)
    tokens = scatter_about(arg_keys[0], (N_REPLICA, TOK_R, D_WIN), 1.0, 6.0, ((0, 8), (1, 4)))
    local_weight = bell_draw_with(arg_keys[1], (N_REPLICA, D_WIN, KVW), 1.0, 6.0, ((0, 8), (1, 4)), (0, 1, 8, 2.0))
    key_cot = scatter_about(arg_keys[2], (N_REPLICA, TOK_R, KVW), 1.0, 6.0, ((0, 8), (1, 4)))
    global_weight = scatter_about(arg_keys[3], (D_WIN, KVW), 1.0, 6.0, ((0, 32),), jnp.float32)
    momentum = scatter_about(arg_keys[4], (D_WIN, KVW), 1.0, 6.0, ((0, 32),), jnp.float32)
    anchor = scatter_about(arg_keys[5], (D_WIN, KVW), 1.0, 6.0, ((0, 32),), jnp.float32)
    return dict(tokens=tokens, local_weight=local_weight, key_cot=key_cot, global_weight=global_weight, momentum=momentum, anchor=anchor)


def reference(tokens, local_weight, key_cot, global_weight, momentum, anchor):
    scale = 1.0 / (D_WIN ** 0.5)

    def worker(items):
        inputs, weight, cot = items
        made = (jnp.dot(inputs, weight, preferred_element_type=jnp.float32) * scale).astype(jnp.bfloat16)
        back = (jnp.dot(cot, weight.T, preferred_element_type=jnp.float32) * scale).astype(jnp.bfloat16)
        wgrad = (jnp.dot(inputs.T, cot, preferred_element_type=jnp.float32) * scale).astype(jnp.bfloat16)
        return made, back, wgrad

    keys, grad_tokens, grad_weight = lax.map(worker, (tokens, local_weight, key_cot))
    total = jnp.sum(local_weight.astype(jnp.float32), axis=0)
    pseudo = global_weight - total / N_REPLICA
    push = pseudo + 0.1 * (global_weight - anchor)
    momentum_new = 0.9 * momentum + push
    global_new = global_weight - 0.7 * (push + 0.9 * momentum_new)
    synced = global_new.astype(jnp.bfloat16)
    return keys, grad_tokens, grad_weight, momentum_new, global_new, synced
```

```python
import functools

import jax
import jax.numpy as jnp
from jax import lax
from jax.experimental import pallas as pl
from jax.experimental.pallas import tpu as pltpu
from jax.sharding import PartitionSpec as P


def swap(value, axis, bit):
    size = lax.axis_size(axis)
    return lax.ppermute(value, axis, [(i, i ^ (1 << bit)) for i in range(size)])


def bit_of(axis, bit):
    return (lax.axis_index(axis) >> bit) & 1


def levels(axis):
    return lax.axis_size(axis).bit_length() - 1


def pick(blocks, at, index):
    return lax.dynamic_index_in_dim(blocks, index, at, keepdims=False)


def half_orders(count):
    if count < 2:
        return [list(range(count))], []
    tail = list(range(2, count))
    return [[0, 1], [1, 0]], tail


def scatter_sum(weight):
    axis = "replica"
    count = levels(axis)
    heads, tail = half_orders(count)
    rows, cols = weight.shape
    block = rows // lax.axis_size(axis)
    width = cols // len(heads)
    parts = []
    for h, order in enumerate(heads):
        piece = weight.reshape((2,) * count + (block, cols))[..., h * width : (h + 1) * width]
        parts.append(dict(terms=[piece], left=list(range(count))[::-1]))

    def split(part, bit):
        at = part["left"].index(bit)
        mine = bit_of(axis, bit)
        keep = [pick(t, at, mine) for t in part["terms"]]
        give = [pick(t, at, 1 - mine) for t in part["terms"]]
        part["terms"] = keep
        part["left"] = [b for b in part["left"] if b != bit]
        total = give[0].astype(jnp.float32)
        for t in give[1:]:
            total = total + t.astype(jnp.float32)
        return total.astype(jnp.bfloat16)

    for step in range(len(heads[0])):
        gives = [split(p, order[step]) for p, order in zip(parts, heads)]
        for p, order, g in zip(parts, heads, gives):
            p["terms"].append(swap(g, axis, order[step]))
    for bit in tail:
        give = jnp.concatenate([split(p, bit) for p in parts], axis=-1)
        got = swap(give, axis, bit)
        for h, p in enumerate(parts):
            p["terms"].append(got[..., h * width : (h + 1) * width])
    sums = []
    for p in parts:
        total = p["terms"][0].astype(jnp.float32)
        for t in p["terms"][1:]:
            total = total + t.astype(jnp.float32)
        sums.append(total)
    return jnp.concatenate(sums, axis=-1)


def gather_blocks(own):
    axis = "replica"
    count = levels(axis)
    heads, tail = half_orders(count)
    block, cols = own.shape
    width = cols // len(heads)
    have, offsets = own[None], [0]
    for bit in reversed(tail):
        have = jnp.concatenate([have, swap(have, axis, bit)], axis=0)
        offsets = offsets + [o | (1 << bit) for o in offsets]
    parts = []
    for h, order in enumerate(heads):
        parts.append((have[..., h * width : (h + 1) * width], offsets))
    for step in range(len(heads[0])):
        nxt = []
        for (have_h, offs), order in zip(parts, heads):
            bit = order[::-1][step]
            got = swap(have_h, axis, bit)
            nxt.append((jnp.concatenate([have_h, got], axis=0), offs + [o | (1 << bit) for o in offs]))
        parts = nxt
    me = lax.axis_index(axis)
    outs = []
    for have_h, offs in parts:
        place = [0] * len(offs)
        for i, o in enumerate(offs):
            place[o] = i
        ordered = have_h[jnp.array(place)] if place != list(range(len(place))) else have_h
        for b in range(count):
            shaped = ordered.reshape((1 << (count - 1 - b), 2, 1 << b) + have_h.shape[1:])
            shaped = jnp.where(bit_of(axis, b) == 1, shaped[:, ::-1], shaped)
            ordered = shaped.reshape(have_h.shape)
        outs.append(ordered)
    full = jnp.concatenate(outs, axis=-1)
    return full.reshape(-1, cols)


def on_device(tokens, local_weight, key_cot, global_weight, momentum, anchor):
    features = tokens.shape[2]
    scale = 1.0 / features**0.5
    inputs = tokens[0]
    weight = local_weight[0]
    cot = key_cot[0]
    axis = "fsdp"
    depth = levels(axis)
    toks = inputs.shape[0]
    feats = weight.shape[0]

    total = scatter_sum(weight)
    pseudo = global_weight - total / lax.axis_size("replica")
    push = pseudo + 0.1 * (global_weight - anchor)
    momentum_new = 0.9 * momentum + push
    global_new = global_weight - 0.7 * (push + 0.9 * momentum_new)
    synced = gather_blocks(global_new.astype(jnp.bfloat16))

    cots = [(0, cot)]
    for bit in reversed(range(depth)):
        mine = jnp.concatenate([c for _, c in cots], axis=0)
        got = swap(mine, axis, bit)
        n = len(cots)
        cots = cots + [(o | (1 << bit), got[i * toks : (i + 1) * toks]) for i, (o, _) in enumerate(cots)]
    order = [o for o, _ in cots]
    cot_all = jnp.concatenate([c for _, c in cots], axis=0)

    held = [(0, inputs)]
    for bit in range(depth):
        mine = bit_of(axis, bit)
        width_low = feats << 0
        def halves(v):
            cols = v.shape[1]
            shaped = v.reshape(v.shape[0], cols // (2 * feats), 2, feats)
            return shaped
        keep, give = [], []
        for o, v in held:
            pairs = v.shape[1] // (2 * feats)
            k = [lax.dynamic_slice(v, (0, (2 * p + mine) * feats), (toks, feats)) for p in range(pairs)]
            g = [lax.dynamic_slice(v, (0, (2 * p + 1 - mine) * feats), (toks, feats)) for p in range(pairs)]
            keep.append((o, jnp.concatenate(k, axis=1)))
            give.append(jnp.concatenate(g, axis=1))
        got = swap(jnp.concatenate(give, axis=0), axis, bit)
        held = keep + [
            (o | (1 << bit), got[i * toks : (i + 1) * toks]) for i, (o, _) in enumerate(keep)
        ]
    by_offset = dict(held)
    columns_all = jnp.concatenate([by_offset[o] for o in order], axis=0)

    wgrad = lax.dot_general(
        columns_all, cot_all, (((0,), (0,)), ((), ())), preferred_element_type=jnp.float32
    )
    grad_weight = (wgrad * scale).astype(jnp.bfloat16)

    def back(c):
        out = lax.dot_general(c, weight, (((1,), (1,)), ((), ())), preferred_element_type=jnp.float32)
        return (out * scale).astype(jnp.bfloat16)

    rows = {o: None for o in order}
    cot_of = dict(cots)
    pieces = {}
    parted = back(cot_all)
    for i, o in enumerate(order):
        pieces[o] = [(0, parted[i * toks : (i + 1) * toks])]
    for bit in range(depth):
        give_keys = [o for o in pieces if (o >> bit) & 1]
        keep_keys = [o for o in pieces if not (o >> bit) & 1]
        give = jnp.concatenate([v for o in give_keys for _, v in pieces[o]], axis=0)
        got = swap(give, axis, bit)
        n = 0
        for o in give_keys:
            to = o ^ (1 << bit)
            new = []
            for w_off, v in pieces[o]:
                new.append((w_off | (1 << bit), got[n * toks : (n + 1) * toks]))
                n += 1
            pieces[to] = pieces[to] + new
        for o in give_keys:
            del pieces[o]
    me = lax.axis_index(axis)
    grad_tokens = jnp.zeros((toks, features), jnp.bfloat16)
    for w_off, v in pieces[0]:
        grad_tokens = lax.dynamic_update_slice(grad_tokens, v, (0, (me ^ w_off) * feats))

    summed = jnp.dot(columns_all, weight, preferred_element_type=jnp.float32)
    part = {o: [summed[i * toks : (i + 1) * toks]] for i, o in enumerate(order)}
    for bit in range(depth):
        give_keys = [o for o in part if (o >> bit) & 1]
        give = jnp.concatenate([sum(t.astype(jnp.float32) for t in part[o]).astype(jnp.bfloat16) for o in give_keys], axis=0)
        got = swap(give, axis, bit)
        for i, o in enumerate(give_keys):
            part[o ^ (1 << bit)].append(got[i * toks : (i + 1) * toks])
            del part[o]
    keys = (sum(t.astype(jnp.float32) for t in part[0]) * scale).astype(jnp.bfloat16)
    return (keys[None], grad_tokens[None], grad_weight[None], momentum_new, global_new, synced)


def solution(mesh):
    in_specs = (
        P("replica", "fsdp", None),
        P("replica", "fsdp", None),
        P("replica", "fsdp", None),
        P(("fsdp", "replica"), None),
        P(("fsdp", "replica"), None),
        P(("fsdp", "replica"), None),
    )
    out_specs = (
        P("replica", "fsdp", None),
        P("replica", "fsdp", None),
        P("replica", "fsdp", None),
        P(("fsdp", "replica"), None),
        P(("fsdp", "replica"), None),
        P("fsdp", None),
    )
    return jax.shard_map(
        on_device, mesh=mesh, in_specs=in_specs, out_specs=out_specs, check_vma=False
    )
```

```python
import jax
import jax.numpy as jnp
from jax import lax
from jax.experimental import pallas as pl
from jax.experimental.pallas import tpu as pltpu
from jax.sharding import PartitionSpec as P


ANY = pl.BlockSpec(memory_space=pl.ANY)
VMEM = pl.BlockSpec(memory_space=pltpu.VMEM)


def levels(axis):
    return lax.axis_size(axis).bit_length() - 1


def swap(value, axis, mask):
    return lax.ppermute(value, axis, [(i, i ^ mask) for i in range(lax.axis_size(axis))])


def bit_of(axis, bit):
    return (lax.axis_index(axis) >> bit) & 1


def place(axis, along, size, pieces, shape, dtype):
    arrays = [a for a, _ in pieces]
    offsets = [o for _, o in pieces]
    total = sum(len(o) for o in offsets)

    def kernel(*refs):
        ins, out, sem = refs[: len(arrays)], refs[len(arrays)], refs[len(arrays) + 1]
        me = lax.axis_index(axis)
        copies = []
        for ref, offs in zip(ins, offsets):
            for k, off in enumerate(offs):
                if off is None:
                    continue
                start = pl.multiple_of((me ^ off) * size, size)
                at = (pl.ds(start, size), slice(None)) if along == 0 else (slice(None), pl.ds(start, size))
                copies.append(pltpu.make_async_copy(ref.at[k], out.at[at], sem.at[len(copies)]))
        for c in copies:
            c.start()
        for c in copies:
            c.wait()

    return pl.pallas_call(
        kernel,
        out_shape=jax.ShapeDtypeStruct(shape, dtype),
        in_specs=[VMEM] * len(arrays),
        out_specs=ANY,
        scratch_shapes=[pltpu.SemaphoreType.DMA((total,))],
        compiler_params=pltpu.CompilerParams(vmem_limit_bytes=8 << 20),
    )(*arrays)


def add(terms):
    total = terms[0].astype(jnp.float32)
    for t in terms[1:]:
        total = total + t.astype(jnp.float32)
    return total


def pick(blocks, index):
    return lax.dynamic_index_in_dim(blocks, index, 0, keepdims=False)


def block_sum(weight):
    axis = "replica"
    count = levels(axis)
    head = min(count, 2)
    size = lax.axis_size(axis)
    block, cols = weight.shape[0] // size, weight.shape[1]
    fan = 1 << head
    tail_size = size // fan
    blocks = weight.reshape(tail_size, fan, block, cols)
    me = lax.axis_index(axis)
    low = me & (fan - 1)
    terms = [lax.dynamic_index_in_dim(blocks, low, 1, keepdims=False)]
    gives = {m: lax.dynamic_index_in_dim(blocks, low ^ m, 1, keepdims=False) for m in range(fan - 1, 0, -1)}
    for m, g in gives.items():
        terms.append(swap(g, axis, m))
    left = tail_size
    for bit in reversed(range(head, count)):
        left //= 2
        mine = bit_of(axis, bit)
        keep = [pick(t.reshape((2, left) + t.shape[1:]), mine) for t in terms]
        give = add([pick(t.reshape((2, left) + t.shape[1:]), 1 - mine) for t in terms])
        got = swap(give.astype(jnp.bfloat16), axis, 1 << bit)
        terms = keep + [got]
    return add(terms)[0]


def all_blocks(own):
    axis = "replica"
    count = levels(axis)
    head = min(count, 2)
    block, cols = own.shape
    have, offsets = own[None], [0]
    for bit in range(head, count):
        have = jnp.concatenate([have, swap(have, axis, 1 << bit)], axis=0)
        offsets = offsets + [o | (1 << bit) for o in offsets]
    pieces = [(have, offsets)]
    for m in range((1 << head) - 1, 0, -1):
        pieces.append((swap(have, axis, m), [o ^ m for o in offsets]))
    shape = (block * lax.axis_size(axis), cols)
    return place(axis, 0, block, pieces, shape, own.dtype)


def on_device(tokens, local_weight, key_cot, global_weight, momentum, anchor):
  features = tokens.shape[2]
  scale = 1.0 / features**0.5
  inputs = tokens[0]
  weight = local_weight[0]
  cot = key_cot[0]
  axis = "fsdp"
  depth = levels(axis)
  toks = inputs.shape[0]
  feats = weight.shape[0]
  bf16, f32 = jnp.bfloat16, jnp.float32

  total = block_sum(weight)
  pseudo = global_weight - total / lax.axis_size("replica")
  push = pseudo + 0.1 * (global_weight - anchor)
  momentum_new = 0.9 * momentum + push
  global_new = global_weight - 0.7 * (push + 0.9 * momentum_new)
  synced = all_blocks(global_new.astype(bf16))

  cots = {0: cot}
  for bit in reversed(range(depth)):
      offs = list(cots)
      mine = cots[0] if len(offs) == 1 else jnp.concatenate([cots[o] for o in offs], axis=0)
      got = swap(mine, axis, 1 << bit)
      for i, o in enumerate(offs):
          cots[o | (1 << bit)] = got[i * toks : (i + 1) * toks]

  held = {0: inputs}
  for bit in range(depth):
      mine = bit_of(axis, bit)
      keep, give = {}, []
      for o, v in held.items():
          pairs = v.shape[1] // (2 * feats)
          cut = lambda which: jnp.concatenate(
              [lax.dynamic_slice(v, (0, (2 * p + which) * feats), (toks, feats)) for p in range(pairs)], axis=1
          )
          keep[o] = cut(mine)
          give.append(cut(1 - mine))
      got = swap(jnp.concatenate(give, axis=0), axis, 1 << bit)
      held = dict(keep)
      for i, o in enumerate(keep):
          held[o | (1 << bit)] = got[i * toks : (i + 1) * toks]

  order = sorted(held)
  columns_all = jnp.concatenate([held[o] for o in order], axis=0)
  cot_all = jnp.concatenate([cots[o] for o in order], axis=0)
  wgrad = lax.dot_general(columns_all, cot_all, (((0,), (0,)), ((), ())), preferred_element_type=f32)
  grad_weight = (wgrad * scale).astype(bf16)

  def back(c):
      out = lax.dot_general(c, weight, (((1,), (1,)), ((), ())), preferred_element_type=f32)
      return (out * scale).astype(bf16)

  for bit in range(depth):
      step = 1 << bit
      if bit == 0:
          give_offs = [o for o in order if o & 1]
          give = back(jnp.concatenate([cots[o] for o in give_offs], axis=0)).reshape(-1, toks, feats)
          rows = {o: [(back(cots[o])[None], [0])] for o in order if not o & 1}
      else:
          give_offs = [o for o in rows if o & step]
          give = jnp.concatenate([a[k][None] for o in give_offs for a, offs in rows[o] for k in range(len(offs)) if offs[k] is not None], axis=0)
      got = swap(give, axis, step)
      per = got.shape[0] // len(give_offs)
      for i, o in enumerate(give_offs):
          to = o ^ step
          if bit == 0:
              offs_got = [step]
          else:
              offs_got = [f | step for a, offs in rows[o] for f in offs if f is not None]
          if len(give_offs) == 1:
              rows[to] = rows[to] + [(got, offs_got)]
          else:
              rows[to] = rows[to] + [(got, [None] * (i * per) + offs_got + [None] * (got.shape[0] - (i + 1) * per))]
          rows.pop(o, None)
  grad_tokens = place(axis, 1, feats, rows[0], (toks, features), bf16)

  def forward(offs):
      return jnp.dot(jnp.concatenate([held[o] for o in offs], axis=0), weight, preferred_element_type=f32)

  give_offs = [o for o in order if o & 1]
  keep_offs = [o for o in order if not o & 1]
  kept = forward(keep_offs)
  part = {o: [kept[i * toks : (i + 1) * toks]] for i, o in enumerate(keep_offs)}
  give = forward(give_offs).astype(bf16)
  for bit in range(depth):
      step = 1 << bit
      if bit:
          give_offs = [o for o in part if o & step]
          give = jnp.concatenate([add(part[o]).astype(bf16) for o in give_offs], axis=0)
      got = swap(give, axis, step)
      for i, o in enumerate(give_offs):
          part[o ^ step].append(got[i * toks : (i + 1) * toks])
          part.pop(o, None)
  keys = (add(part[0]) * scale).astype(bf16)
  return (keys[None], grad_tokens[None], grad_weight[None], momentum_new, global_new, synced)


def solution(mesh):
    in_specs = (
        P("replica", "fsdp", None),
        P("replica", "fsdp", None),
        P("replica", "fsdp", None),
        P(("fsdp", "replica"), None),
        P(("fsdp", "replica"), None),
        P(("fsdp", "replica"), None),
    )
    out_specs = (
        P("replica", "fsdp", None),
        P("replica", "fsdp", None),
        P("replica", "fsdp", None),
        P(("fsdp", "replica"), None),
        P(("fsdp", "replica"), None),
        P("fsdp", None),
    )
    return jax.shard_map(
        on_device, mesh=mesh, in_specs=in_specs, out_specs=out_specs, check_vma=False
    )
```
